32 devices in a mesh: grp: 2 (over x), seq: 16 (over z, y, core).
Axes of the slice: x: 2, y: 2, z: 4, core: 2. Of those that a mesh axis runs over, the one named last changes fastest.
Arguments:
- queries: bfloat16 [6144, 4096], P(('grp', 'seq')), parts along dimension 0, may hold values from -6 to 6
- keys: bfloat16 [6144, 4096], P(('grp', 'seq')), parts along dimension 0, may hold values from -6 to 6
- values: bfloat16 [6144, 4096], P(('grp', 'seq')), parts along dimension 0, may hold values from -6 to 6
- latent_in: float32 [6144, 64], P(('grp', 'seq')), parts along dimension 0, may hold values from -6 to 6
- mod_table: float32 [16, 2, 4096], replicated, may hold values from -3 to 3
- step_size: float32 [16], replicated, may hold values from 0.25 to 1
- timestep: int32 [64], P('grp'), parts along dimension 0, may hold values from 0 to 15
- head_weight: float32 [4096, 64], replicated, may hold values from -0.09375 to 0.09375
- conv_in_weight: bfloat16 [27, 16, 384], replicated, may hold values from -0.3125 to 0.3125
- conv_in_bias: float32 [384], replicated, may hold values from -3 to 3
- norm_gain: float32 [384], replicated, may hold values from 0.1 to 1.9
- conv_weight: bfloat16 [27, 384, 384], replicated, may hold values from -0.0625 to 0.0625
- conv_bias: float32 [384], replicated, may hold values from -3 to 3
- patch_weight: bfloat16 [1536, 1024], replicated, may hold values from -0.15625 to 0.15625
- patch_gain: float32 [1024], replicated, may hold values from 0.1 to 1.9
- post_gain: float32 [1024], replicated, may hold values from 0.1 to 1.9
- proj_weight: float32 [1024, 768], replicated, may hold values from -0.1875 to 0.1875
- text_table: bfloat16 [24704, 768], P(None, 'seq'), may hold values from -6 to 6
- prompt_ids: int32 [154], P('grp'), parts along dimension 0, may hold values from 0 to 24703
- frame_order: int32 [64], P('grp'), parts along dimension 0, may hold values from 0 to 31, each once
Outputs:
- latent_next: float32 [6144, 64], P(('grp', 'seq')), parts along dimension 0
- decoded: bfloat16 [64, 16, 24, 384], P(('grp', 'seq')), parts along dimension 0
- image_embed: float32 [64, 768], P(('grp', 'seq')), parts along dimension 0
- scores: float32 [64], P(('grp', 'seq')), parts along dimension 0
The draws below stay inside these ranges and needn't reach their ends.
There are 2 independent parts, one for each index of `grp`. The reference program is written for one: setup_inputs(seed, part) draws one part's arguments, and reference() takes and returns one part's arrays. A program takes and returns all parts, laid end to end along the dimension named above; an argument that names none is the same for every part. Nothing has to cross between parts.
All inputs are finite; a program needn't handle non-finite values.
Results may differ from the reference program's by a relative error of at most 0.009.
Values may be sent and summed in bfloat16 or wider, within the bound.
A program may use at most 128 MiB of HBM per device.

```python
import jax
import jax.numpy as jnp
from jax import lax

GRID_H = 8
GRID_W = 12
HEADS = 32
HD = 128
LAT_C = 16
CH = 384
VIT_W = 1024
TEXT_W = 768
VOCAB = 24704
PROMPT = 77
STEPS = 16
FRAMES = 32
TOKENS = 3072


def backdrop(key):
    canvas = jnp.clip(jax.random.normal(key, (TOKENS, HEADS * HD), jnp.float32), -6.0, 6.0)
    return canvas


def draw_queries(key, part):
    canvas = backdrop(jax.random.fold_in(key, 11))
    return canvas.astype(jnp.bfloat16)


def draw_keys(key, part):
    canvas = backdrop(jax.random.fold_in(key, 12))
    return canvas.astype(jnp.bfloat16)


def touch_ends(drawn, own_key, least, largest):
    longest = drawn.shape.index(max(drawn.shape))
    spots = []
    for shift in (0, 1):
        where = [jax.random.randint(jax.random.fold_in(own_key, axis), (), 0, length) for axis, length in enumerate(drawn.shape)]
        where[longest] = (where[longest] + shift) % drawn.shape[longest]
        spots.append(tuple(where))
    return drawn.at[spots[0]].set(least).at[spots[1]].set(largest)


def block_levels(key, shape, cuts, smallest, high):
    loudness = 1.0
    for axis_at, shards_of in cuts:
        draws = jax.random.uniform(jax.random.fold_in(jax.random.fold_in(key, 6), axis_at), (shards_of,), jnp.float32, smallest / len(cuts), high / len(cuts))
        loudness = loudness * jnp.repeat(jnp.exp(draws), shape[axis_at] // shards_of).reshape((-1,) + (1,) * (len(shape) - 1 - axis_at))
    return loudness


def scatter_about(own_key, dims, deviation, limit, shards=(), held_as=jnp.bfloat16):
    gain = block_levels(own_key, dims, shards, -0.22, 0.18) if shards else 1.0
    drawn = jax.random.normal(own_key, dims, jnp.float32) * deviation * gain
    return jnp.minimum(jnp.maximum(drawn, -limit), limit).astype(held_as)


def setup_inputs(seed: int = 0, part: int = 0) -> dict:
    key_list = jax.random.split(jax.random.key(seed), 21)
    own_keys = jax.random.split(jax.random.fold_in(key_list[20], part), 21)
    queries = draw_queries(jax.random.fold_in(jax.random.fold_in(key_list[20], part), 71), part)
    keys = draw_keys(jax.random.fold_in(jax.random.fold_in(key_list[20], part), 71), part)
    values = scatter_about(own_keys[2], (TOKENS, HEADS * HD), 1.0, 6.0, ((0, 16),))
    latent_in = scatter_about(own_keys[3], (TOKENS, 4 * LAT_C), 1.0, 6.0, ((0, 16),), jnp.float32)
    mod_table = scatter_about(key_list[4], (STEPS, 2, HEADS * HD), 0.5, 3.0, (), jnp.float32)
    step_size = jnp.clip(jax.random.uniform(key_list[5], (STEPS,), jnp.float32, 0.25, 1.0), 0.25, 1.0)
    timestep = touch_ends(jax.random.randint(own_keys[6], (FRAMES,), 0, STEPS), jax.random.fold_in(own_keys[6], 1), 0, STEPS - 1).astype(jnp.int32)
    head_weight = scatter_about(key_list[7], (HEADS * HD, 4 * LAT_C), (HEADS * HD) ** -0.5, 0.09375, (), jnp.float32)
    conv_in_weight = scatter_about(key_list[8], (27, LAT_C, CH), (27 * LAT_C) ** -0.5, 0.3125)
    conv_in_bias = scatter_about(key_list[9], (CH,), 0.5, 3.0, (), jnp.float32)
    norm_gain = jnp.clip(1.0 + 0.18 * jax.random.normal(key_list[10], (CH,), jnp.float32), 0.1, 1.9)
    conv_weight = scatter_about(key_list[11], (27, CH, CH), (27 * CH) ** -0.5, 0.0625)
    conv_bias = scatter_about(key_list[12], (CH,), 0.5, 3.0, (), jnp.float32)
    patch_weight = scatter_about(key_list[13], (4 * CH, VIT_W), (4 * CH) ** -0.5, 0.15625)
    patch_gain = jnp.clip(1.0 + 0.18 * jax.random.normal(key_list[14], (VIT_W,), jnp.float32), 0.1, 1.9)
    post_gain = jnp.clip(1.0 + 0.18 * jax.random.normal(key_list[15], (VIT_W,), jnp.float32), 0.1, 1.9)
    proj_weight = scatter_about(key_list[16], (VIT_W, TEXT_W), VIT_W ** -0.5, 0.1875, (), jnp.float32)
    text_table = scatter_about(key_list[17], (VOCAB, TEXT_W), 1.0, 6.0, ((1, 16),))
    prompt_ids = touch_ends(jax.random.randint(own_keys[18], (PROMPT,), 0, VOCAB), jax.random.fold_in(own_keys[18], 1), 0, VOCAB - 1).astype(jnp.int32)
    frame_order = jax.random.permutation(own_keys[19], FRAMES).astype(jnp.int32)
    return dict(queries=queries, keys=keys, values=values, latent_in=latent_in, mod_table=mod_table, step_size=step_size, timestep=timestep, head_weight=head_weight, conv_in_weight=conv_in_weight, conv_in_bias=conv_in_bias, norm_gain=norm_gain, conv_weight=conv_weight, conv_bias=conv_bias, patch_weight=patch_weight, patch_gain=patch_gain, post_gain=post_gain, proj_weight=proj_weight, text_table=text_table, prompt_ids=prompt_ids, frame_order=frame_order)


highest = lax.Precision.HIGHEST

def lookup(mod_table, step_size, timestep):
    onehot = (jnp.arange(mod_table.shape[0], dtype=jnp.int32)[None, :] == timestep[:, None]).astype(jnp.float32)
    modulation = jnp.dot(onehot, mod_table.reshape(mod_table.shape[0], -1), precision=highest)
    return (modulation[:, :HEADS * HD], modulation[:, HEADS * HD:], lax.optimization_barrier(jnp.sum(onehot * step_size[None, :], axis=1)))

def attend(queries, keys, values):
    length = queries.shape[0]
    block_rows = 512 if length % 512 == 0 else length

    def split_heads(matrix):
        return matrix.reshape(length, HEADS, HD).transpose(1, 0, 2)

    def one_head(triple):
        head_q, head_k, head_v = triple

        def one_block(rows_q):
            logits = jnp.dot(rows_q, head_k.T, preferred_element_type=jnp.float32) * HD ** (-0.5)
            row_peak = lax.optimization_barrier(jnp.max(logits, axis=-1, keepdims=True))
            exponent = jnp.exp(logits - row_peak)
            weights = (exponent / lax.optimization_barrier(jnp.sum(exponent, axis=-1, keepdims=True))).astype(jnp.bfloat16)
            return jnp.dot(weights, head_v, preferred_element_type=jnp.float32).astype(jnp.bfloat16)
        return lax.map(one_block, head_q.reshape(length // block_rows, block_rows, HD)).reshape(length, HD)
    heads_out = lax.map(one_head, (split_heads(queries), split_heads(keys), split_heads(values)))
    return heads_out.transpose(1, 0, 2).reshape(length, HEADS * HD)

def predict(attended, mod_shift, mod_scale, head_weight):
    frames_n = mod_shift.shape[0]
    attended_f = attended.astype(jnp.float32)
    meansq = lax.optimization_barrier(jnp.mean(attended_f * attended_f, axis=-1, keepdims=True))
    normed = (attended_f * lax.rsqrt(meansq + 1e-06)).reshape(frames_n, -1, attended.shape[1])
    normed = normed * (1.0 + mod_scale[:, None, :]) + mod_shift[:, None, :]
    return jnp.dot(normed.reshape(attended.shape[0], -1), head_weight, precision=highest)

def advance(latent_in, step_dt, prediction):
    frames_n = step_dt.shape[0]
    shaped = latent_in.reshape(frames_n, -1, latent_in.shape[1]) + step_dt[:, None, None] * prediction.reshape(frames_n, -1, latent_in.shape[1])
    return shaped.reshape(latent_in.shape)

def to_frames(latent):
    shaped = latent.reshape(-1, GRID_H, GRID_W, 2, 2, LAT_C).transpose(0, 1, 3, 2, 4, 5)
    return shaped.reshape(-1, 2 * GRID_H, 2 * GRID_W, LAT_C)

def causal_conv(padded, weight):
    frames_n = padded.shape[0] - 2
    rows_h = padded.shape[1]
    cols_w = padded.shape[2]
    spaced = jnp.pad(padded, ((0, 0), (1, 1), (1, 1), (0, 0)))
    summed = jnp.zeros((frames_n * rows_h * cols_w, weight.shape[2]), jnp.float32)
    for lag_t in range(3):
        for row_off in range(3):
            for col_off in range(3):
                window = spaced[lag_t:lag_t + frames_n, row_off:row_off + rows_h, col_off:col_off + cols_w]
                window = window.reshape(-1, spaced.shape[3])
                summed = summed + jnp.dot(window, weight[lag_t * 9 + row_off * 3 + col_off], preferred_element_type=jnp.float32)
    return summed.reshape(frames_n, rows_h, cols_w, weight.shape[2])

def activate(first_out, norm_gain):
    first_f = first_out.astype(jnp.float32)
    meansq = lax.optimization_barrier(jnp.mean(first_f * first_f, axis=-1, keepdims=True))
    return jax.nn.silu(first_f * lax.rsqrt(meansq + 1e-06) * norm_gain).astype(jnp.bfloat16)

def to_patches(decoded):
    shaped = decoded.reshape(-1, GRID_H, 2, GRID_W, 2, CH).transpose(0, 1, 3, 2, 4, 5)
    return shaped.reshape(-1, GRID_H * GRID_W, 4 * CH)

def embed(patches, patch_weight):
    flat_rows = patches.reshape(-1, patches.shape[2])
    product = jnp.dot(flat_rows, patch_weight, preferred_element_type=jnp.float32)
    return product.reshape(patches.shape[0], patches.shape[1], -1).astype(jnp.bfloat16)

def layer_norm(matrix, gain_vec):
    centered = matrix - lax.optimization_barrier(jnp.mean(matrix, axis=-1, keepdims=True))
    variance = lax.optimization_barrier(jnp.mean(centered * centered, axis=-1, keepdims=True))
    return centered * lax.rsqrt(variance + 1e-05) * gain_vec

def describe(embedded, patch_gain, post_gain, proj_weight):
    pooled = lax.optimization_barrier(jnp.mean(layer_norm(embedded.astype(jnp.float32), patch_gain), axis=-2))
    return jnp.dot(layer_norm(pooled, post_gain), proj_weight, precision=highest)

def rate(image_vec, text_vector):
    inner = lax.optimization_barrier(jnp.sum(image_vec * text_vector[None, :], axis=-1))
    image_rms = jnp.sqrt(lax.optimization_barrier(jnp.mean(image_vec * image_vec, axis=-1)) + 1e-06)
    text_rms = jnp.sqrt(jnp.mean(text_vector * text_vector) + 1e-06)
    return 100.0 * inner / (TEXT_W * image_rms * text_rms)

def reference(queries, keys, values, latent_in, mod_table, step_size, timestep, head_weight, conv_in_weight, conv_in_bias, norm_gain, conv_weight, conv_bias, patch_weight, patch_gain, post_gain, proj_weight, text_table, prompt_ids, frame_order):
    mod_shift, mod_scale, step_dt = lookup(mod_table, step_size, timestep)
    attended = attend(queries, keys, values)
    latent_next = advance(latent_in, step_dt, predict(attended, mod_shift, mod_scale, head_weight))
    frames = to_frames(latent_next).astype(jnp.bfloat16)
    zeros_lat = jnp.zeros((2,) + frames.shape[1:], jnp.bfloat16)
    first_out = (causal_conv(jnp.concatenate([zeros_lat, frames], axis=0), conv_in_weight) + conv_in_bias).astype(jnp.bfloat16)
    activated = activate(first_out, norm_gain)
    zeros_act = jnp.zeros((2,) + activated.shape[1:], jnp.bfloat16)
    branch = causal_conv(jnp.concatenate([zeros_act, activated], axis=0), conv_weight)
    decoded = (branch + conv_bias + first_out.astype(jnp.float32)).astype(jnp.bfloat16)
    image_vec = describe(embed(to_patches(decoded), patch_weight), patch_gain, post_gain, proj_weight)
    text_vector = lax.optimization_barrier(jnp.mean(jnp.take(text_table, prompt_ids, axis=0).astype(jnp.float32), axis=0))
    image_embed = jnp.take(image_vec, frame_order, axis=0)
    return (latent_next, decoded, image_embed, rate(image_embed, text_vector))
```

```python
import functools

import jax
import jax.numpy as jnp
from jax import lax
from jax.experimental import pallas as pl
from jax.experimental.pallas import tpu as pltpu
from jax.sharding import PartitionSpec as P

GRID_H = 8
GRID_W = 12
HEADS = 32
HD = 128
LAT_C = 16
CH = 384
TEXT_W = 768


highest = lax.Precision.HIGHEST


def shifted(value, axis, steps):
    count = lax.axis_size(axis)
    initial, last = (max(0, -steps), min(count, count - steps))
    return lax.ppermute(value, axis, [(source, source + steps) for source in range(initial, last)])


def lookup(mod_table, step_size, timestep):
    onehot = (jnp.arange(mod_table.shape[0], dtype=jnp.int32)[None, :] == timestep[:, None]).astype(
        jnp.float32
    )
    modulation = jnp.dot(onehot, mod_table.reshape(mod_table.shape[0], -1), precision=highest)
    return (
        modulation[:, : HEADS * HD],
        modulation[:, HEADS * HD :],
        jnp.sum(onehot * step_size[None, :], axis=1),
    )


def attend_kernel(q_ref, k_ref, v_ref, out_ref):
    sources, _, rows, width = k_ref.shape
    head_k = k_ref[...].reshape(sources * rows, width)
    head_v = v_ref[...].reshape(sources * rows, width)
    for part in range(q_ref.shape[0]):
        logits = lax.dot_general(
            q_ref[part, 0], head_k, (((1,), (1,)), ((), ())), preferred_element_type=jnp.float32
        )
        row_peak = jnp.max(logits, axis=-1, keepdims=True)
        exponent = jnp.exp2((logits - row_peak) * (HD ** (-0.5) * 1.4426950408889634))
        total = jnp.sum(exponent, axis=-1, keepdims=True)
        mixed = jnp.dot(exponent.astype(jnp.bfloat16), head_v, preferred_element_type=jnp.float32)
        out_ref[part] = (mixed / total).astype(jnp.bfloat16)


def attend_head(packed):
    sources, _, rows, width = packed.shape
    length = sources * rows
    step = 2 if sources % 2 == 0 else 1
    whole = (sources, 1, rows, width)
    return pl.pallas_call(
        attend_kernel,
        grid=(sources // step,),
        in_specs=[
            pl.BlockSpec((step, 1, rows, width), lambda i: (i, 0, 0, 0)),
            pl.BlockSpec(whole, lambda i: (0, 1, 0, 0)),
            pl.BlockSpec(whole, lambda i: (0, 2, 0, 0)),
        ],
        out_specs=pl.BlockSpec((step, rows, width), lambda i: (i, 0, 0)),
        out_shape=jax.ShapeDtypeStruct((sources, rows, width), jnp.bfloat16),
        cost_estimate=pl.CostEstimate(
            flops=4 * length * length * width,
            bytes_accessed=8 * length * width,
            transcendentals=length * length,
        ),
        name="attend",
    )(packed, packed, packed)


def advance_kernel(heads_here, *refs):
    parts = refs[:heads_here]
    scale_ref, weight_ref, shift_ref, step_ref, latent_ref, out_ref = refs[heads_here:]
    sources, rows, width = parts[0].shape
    frames_n = scale_ref.shape[0]

    def one_source(source, carry):
        summed, squares = carry
        for local_head in range(heads_here):
            head = source * heads_here + local_head
            rows_f = parts[local_head][source].astype(jnp.float32)
            squares = squares + rows_f * rows_f
            gain = 1.0 + scale_ref[:, pl.ds(pl.multiple_of(head * width, width), width)]
            scaled = rows_f.reshape(frames_n, -1, width) * gain[:, None, :]
            summed = summed + jnp.dot(
                scaled.reshape(rows, width),
                weight_ref[head],
                precision=highest,
                preferred_element_type=jnp.float32,
            )
        return summed, squares

    summed, squares = lax.fori_loop(
        0,
        sources,
        one_source,
        (jnp.zeros(out_ref.shape, jnp.float32), jnp.zeros((rows, width), jnp.float32)),
    )
    meansq = jnp.sum(squares, axis=-1, keepdims=True) / (sources * heads_here * width)
    prediction = (summed * lax.rsqrt(meansq + 1e-06)).reshape(frames_n, -1, out_ref.shape[1])
    prediction = prediction + shift_ref[...][:, None, :]
    moved = (step_ref[...][:, None, :] * prediction).reshape(out_ref.shape)
    out_ref[...] = latent_ref[...] + moved


def advance(parts, scale_own, head_weight, shift_own, step_own, latent_in):
    shift_part = jnp.dot(shift_own, head_weight, precision=highest)
    step_wide = jnp.broadcast_to(step_own[:, None], shift_part.shape)
    return pl.pallas_call(
        functools.partial(advance_kernel, len(parts)),
        out_shape=jax.ShapeDtypeStruct(latent_in.shape, jnp.float32),
        name="advance",
    )(
        *parts,
        scale_own,
        head_weight.reshape(HEADS, HD, head_weight.shape[1]),
        shift_part,
        step_wide,
        latent_in,
    )


def to_frames(latent):
    shaped = latent.reshape(-1, GRID_H, GRID_W, 2, 2, LAT_C).transpose(0, 1, 3, 2, 4, 5)
    return shaped.reshape(-1, 2 * GRID_H, 2 * GRID_W, LAT_C)


def causal_conv(padded, weight):
    frames_n = padded.shape[0] - 2
    rows_h = padded.shape[1]
    cols_w = padded.shape[2]
    spaced = jnp.pad(padded, ((0, 0), (1, 1), (1, 1), (0, 0)))
    summed = jnp.zeros((frames_n * rows_h * cols_w, weight.shape[2]), jnp.float32)
    for lag_t in range(3):
        for row_off in range(3):
            for col_off in range(3):
                window = spaced[
                    lag_t : lag_t + frames_n, row_off : row_off + rows_h, col_off : col_off + cols_w
                ]
                window = window.reshape(-1, spaced.shape[3])
                summed = summed + jnp.dot(
                    window,
                    weight[lag_t * 9 + row_off * 3 + col_off],
                    preferred_element_type=jnp.float32,
                )
    return summed.reshape(frames_n, rows_h, cols_w, weight.shape[2])


def activate(first_out, norm_gain):
    first_f = first_out.astype(jnp.float32)
    meansq = jnp.mean(first_f * first_f, axis=-1, keepdims=True)
    return jax.nn.silu(first_f * lax.rsqrt(meansq + 1e-06) * norm_gain).astype(jnp.bfloat16)


def to_patches(decoded):
    shaped = decoded.reshape(-1, GRID_H, 2, GRID_W, 2, CH).transpose(0, 1, 3, 2, 4, 5)
    return shaped.reshape(-1, GRID_H * GRID_W, 4 * CH)


def embed(patches, patch_weight):
    flat_rows = patches.reshape(-1, patches.shape[2])
    product = jnp.dot(flat_rows, patch_weight, preferred_element_type=jnp.float32)
    return product.reshape(patches.shape[0], patches.shape[1], -1).astype(jnp.bfloat16)


def layer_norm(matrix, gain_vec):
    centered = matrix - jnp.mean(matrix, axis=-1, keepdims=True)
    variance = jnp.mean(centered * centered, axis=-1, keepdims=True)
    return centered * lax.rsqrt(variance + 1e-05) * gain_vec


def describe(embedded, patch_gain, post_gain, proj_weight):
    pooled = jnp.mean(layer_norm(embedded.astype(jnp.float32), patch_gain), axis=-2)
    return jnp.dot(layer_norm(pooled, post_gain), proj_weight, precision=highest)


def rate(image_vec, text_vector):
    inner = jnp.sum(image_vec * text_vector[None, :], axis=-1)
    image_rms = jnp.sqrt(jnp.mean(image_vec * image_vec, axis=-1) + 1e-06)
    text_rms = jnp.sqrt(jnp.mean(text_vector * text_vector) + 1e-06)
    return 100.0 * inner / (TEXT_W * image_rms * text_rms)


def local(
    queries,
    keys,
    values,
    latent_in,
    mod_table,
    step_size,
    timestep,
    head_weight,
    conv_in_weight,
    conv_in_bias,
    norm_gain,
    conv_weight,
    conv_bias,
    patch_weight,
    patch_gain,
    post_gain,
    proj_weight,
    text_table,
    prompt_ids,
    frame_order,
):
    tokens_dev = queries.shape[0]
    frames_dev = tokens_dev // (GRID_H * GRID_W)
    devices = lax.axis_size("seq")
    first_frame = lax.axis_index("seq") * frames_dev
    shift_own, scale_own, step_own = lookup(
        mod_table, step_size, lax.dynamic_slice_in_dim(timestep, first_frame, frames_dev, 0)
    )
    heads_here = HEADS // devices

    def exchange(matrix):
        return lax.all_to_all(matrix, "seq", split_axis=0, concat_axis=0, tiled=True)

    def one_head(matrix, local_head):
        columns = [
            matrix[:, (owner * heads_here + local_head) * HD :][:, :HD] for owner in range(devices)
        ]
        return jnp.stack(columns, axis=0)

    packed = [
        exchange(jnp.stack([one_head(m, local_head) for m in (queries, keys, values)], axis=1))
        for local_head in range(heads_here)
    ]
    parts = [exchange(attend_head(one)) for one in packed]
    latent_next = advance(parts, scale_own, head_weight, shift_own, step_own, latent_in)
    frames = to_frames(latent_next).astype(jnp.bfloat16)
    frames_near = shifted(frames, "seq", 1)
    frames_far = shifted(frames, "seq", 2)
    stacked = jnp.concatenate([frames_far, frames_near, frames], axis=0)
    first_wide = (causal_conv(stacked, conv_in_weight) + conv_in_bias).astype(jnp.bfloat16)
    first_out = first_wide[2:]
    frame_ids = (
        lax.axis_index("seq") * frames.shape[0]
        - 2
        + jnp.arange(frames.shape[0] + 2, dtype=jnp.int32)
    )
    widened = jnp.where(
        (frame_ids >= 0)[:, None, None, None],
        activate(first_wide, norm_gain),
        jnp.zeros((), jnp.bfloat16),
    )
    branch = causal_conv(widened, conv_weight)
    decoded = (branch + conv_bias + first_out.astype(jnp.float32)).astype(jnp.bfloat16)
    own_text = jnp.mean(jnp.take(text_table, prompt_ids, axis=0).astype(jnp.float32), axis=0)
    patches = to_patches(decoded)
    image_src = describe(embed(patches, patch_weight), patch_gain, post_gain, proj_weight)
    bundle = jnp.concatenate([image_src.reshape(-1), own_text])
    gathered = exchange(jnp.broadcast_to(bundle[None, :], (devices, bundle.shape[0])))
    images = gathered[:, : image_src.size].reshape(-1, image_src.shape[1])
    text_vector = gathered[:, image_src.size :].reshape(-1)
    order_own = lax.dynamic_slice_in_dim(frame_order, first_frame, frames_dev, 0)
    image_vec = jnp.take(images, order_own, axis=0, mode="clip")
    return (latent_next, decoded, image_vec, rate(image_vec, text_vector))


def solution(mesh):
    in_specs = (
        P(("grp", "seq"), None),
        P(("grp", "seq"), None),
        P(("grp", "seq"), None),
        P(("grp", "seq"), None),
        P(),
        P(),
        P("grp"),
        P(),
        P(),
        P(),
        P(),
        P(),
        P(),
        P(),
        P(),
        P(),
        P(),
        P(None, "seq"),
        P("grp"),
        P("grp"),
    )
    out_specs = (
        P(("grp", "seq"), None),
        P(("grp", "seq"), None, None, None),
        P(("grp", "seq"), None),
        P(("grp", "seq")),
    )
    return jax.shard_map(local, mesh=mesh, in_specs=in_specs, out_specs=out_specs, check_vma=False)
```
